32 devices in a mesh: dp: 4 (over y, core), expert: 8 (over z, x).
Axes of the slice: x: 2, y: 2, z: 4, core: 2. Of those that a mesh axis runs over, the one named last changes fastest.
Arguments:
- tokens: bfloat16 [4096, 2048], P(('dp', 'expert'))
- gain: float32 [2048], replicated, may hold values from 0.25 to 1.75
- gates: float32 [4096, 4], P(('dp', 'expert')), may hold values from 0.1 to 0.5
- expert_ids: int32 [4096, 4], P(('dp', 'expert')), may hold values from 0 to 31, as said below
- w_gate: bfloat16 [32, 2048, 768], P(('dp', 'expert')), may hold values from -0.125 to 0.125
- w_up: bfloat16 [32, 2048, 768], P(('dp', 'expert')), may hold values from -0.125 to 0.125
- w_down: bfloat16 [32, 768, 2048], P(('dp', 'expert')), may hold values from -0.21875 to 0.21875
- grad_out: bfloat16 [4096, 2048], P(('dp', 'expert'))
Outputs:
- moe_out: bfloat16 [4096, 2048], P(('dp', 'expert'))
- token_gradient: bfloat16 [4096, 2048], P(('dp', 'expert'))
- grad_gates: float32 [4096, 4], P(('dp', 'expert'))
- gain_gradient: float32 [2048], replicated
- grad_w_gate: bfloat16 [32, 2048, 768], P(('dp', 'expert'))
- grad_w_up: bfloat16 [32, 2048, 768], P(('dp', 'expert'))
- grad_w_down: bfloat16 [32, 768, 2048], P(('dp', 'expert'))
The draws below stay inside these ranges and needn't reach their ends.
Inputs may be any that keep to these rules, and one draw needn't show every extreme that they name: `expert_ids`: A token's 4 ids name distinct experts; the tokens of one device (aligned blocks of 128 rows) name no expert more than 32 times, and some expert exactly 32 times.
All inputs are finite; a program needn't handle non-finite values.
Results may differ from the reference program's by a relative error of at most 0.008.
Values may be sent and summed in bfloat16 or wider, within the bound.
No kernel may reach another device: no remote copies, remote signals or barrier semaphores. Data moves between devices by JAX's collectives and lax.ppermute only.
A program may use at most 128 MiB of HBM per device.

```python
import math
import jax
import jax.numpy as jnp
from jax import lax

D = 2048
FF = 768
TOK_DEV = 128
TOP = 4
EXPERTS = 32
TOKENS = 4096
CAP = 32


def draw_tokens(key, part):
    key_base, key_row, key_col = jax.random.split(key, 3)
    base_values = jax.random.normal(key_base, (TOKENS, D), jnp.float32)
    row_scale = jnp.exp(jax.random.uniform(key_row, (TOKENS, 1), jnp.float32, math.log(0.3), math.log(3.0)))
    col_scale = jnp.exp(jax.random.uniform(key_col, (1, D), jnp.float32, math.log(0.3), math.log(3.0)))
    values = row_scale * col_scale * base_values
    return values.astype(jnp.bfloat16)


def draw_grad_out(key, part):
    key_base = jax.random.fold_in(key, 0)
    position = jnp.arange(TOKENS, dtype=jnp.float32)[:, None] / (TOKENS - 1)
    rising = 1.0 + 2.0 * position
    values = rising * jax.random.normal(key_base, (TOKENS, D), jnp.float32)
    return values.astype(jnp.bfloat16)


def draw_expert_ids(key, part):
    quarter = EXPERTS // 4
    step_size = CAP // 4
    hottest = jax.random.randint(jax.random.fold_in(key, 7), (), 0, EXPERTS).astype(jnp.int32)

    def block_ids(block_key):
        key_first, key_second, key_perm, key_rows = jax.random.split(block_key, 4)
        shift_first = jax.random.randint(key_first, (quarter,), 0, step_size + 1).astype(jnp.int32).at[0].set(0)
        shift_second = jax.random.randint(key_second, (quarter,), 0, step_size + 1).astype(jnp.int32)
        template = jnp.concatenate([CAP - shift_first, CAP // 2 - shift_second, step_size + shift_second, step_size + shift_first]).astype(jnp.int32)
        others = (hottest + 1 + jax.random.permutation(key_perm, EXPERTS - 1).astype(jnp.int32)) % EXPERTS
        ordering = jnp.concatenate([hottest[None], others]).astype(jnp.int32)
        counts = jnp.zeros((EXPERTS,), jnp.int32).at[ordering].set(template)
        bounds = jnp.cumsum(counts).astype(jnp.int32)
        listing = jnp.searchsorted(bounds, jnp.arange(TOK_DEV * TOP, dtype=jnp.int32), side='right').astype(jnp.int32)
        table = listing.reshape(TOP, TOK_DEV).T
        return table[jax.random.permutation(key_rows, TOK_DEV)]

    def block_key_of(index):
        return jax.random.fold_in(key, index + 11)
    block_keys = jax.vmap(block_key_of)(jnp.arange(TOKENS // TOK_DEV, dtype=jnp.int32))
    blocks = jax.vmap(block_ids)(block_keys)
    return blocks.reshape(TOKENS, TOP).astype(jnp.int32)


def levels(key, shape, shards, smallest, top_value):
    level = 1.0
    for dim, blocks in shards:
        steps = jax.random.uniform(jax.random.fold_in(jax.random.fold_in(key, 6), dim), (blocks,), jnp.float32, smallest / len(shards), top_value / len(shards))
        level = level * jnp.repeat(jnp.exp(steps), shape[dim] // blocks).reshape((-1,) + (1,) * (len(shape) - 1 - dim))
    return level


def noise(rng, extent, width, most, cuts=(), kind=jnp.bfloat16):
    loudness = levels(rng, extent, cuts, -0.22, 0.18) if cuts else 1.0
    entries = jax.random.normal(rng, extent, jnp.float32) * width * loudness
    return jnp.minimum(jnp.maximum(entries, -most), most).astype(kind)


def setup_inputs(seed: int = 0) -> dict:
    streams_of = jax.random.split(jax.random.key(seed), 9)
    return {
        "tokens": draw_tokens(jax.random.fold_in(streams_of[8], 71), 0),
        "gain": jnp.clip(1.0 + 0.15 * jax.random.normal(streams_of[1], (D,), jnp.float32), 0.25, 1.75),
        "gates": jnp.clip(jnp.exp(math.log(0.5) - 1.609438 * jax.random.uniform(streams_of[2], (TOKENS, TOP), jnp.float32) ** levels(streams_of[2], (TOKENS, TOP), ((0, 32),), -0.2, 0.2)), 0.1, 0.5),
        "expert_ids": draw_expert_ids(jax.random.fold_in(streams_of[8], 71), 0),
        "w_gate": noise(streams_of[4], (EXPERTS, D, FF), D ** -0.5, 0.125, ((0, 32),)),
        "w_up": noise(streams_of[5], (EXPERTS, D, FF), D ** -0.5, 0.125, ((0, 32),)),
        "w_down": noise(streams_of[6], (EXPERTS, FF, D), FF ** -0.5, 0.21875, ((0, 32),)),
        "grad_out": draw_grad_out(jax.random.fold_in(streams_of[8], 71), 0),
    }


def reference(tokens, gain, gates, expert_ids, w_gate, w_up, w_down, grad_out):
    widened_float = tokens.astype(jnp.float32)
    inverse_root_mean = lax.rsqrt(lax.optimization_barrier(jnp.mean(widened_float * widened_float, axis=1, keepdims=True)) + 1e-06)
    unit_scaled_input = widened_float * inverse_root_mean
    normalized_tokens = (unit_scaled_input * gain).astype(jnp.bfloat16)
    cotangent = grad_out.astype(jnp.float32)
    row_count = EXPERTS * CAP

    def per_expert(totals, expert_slot):
        out_sum, grad_sum, gate_grad = totals
        matches = expert_ids == expert_slot
        is_named = jnp.any(matches, axis=1)
        picked = jnp.nonzero(is_named, size=row_count, fill_value=0)[0].astype(jnp.int32)
        is_live = jnp.arange(row_count, dtype=jnp.int32) < jnp.sum(is_named.astype(jnp.int32))
        live_float = is_live.astype(jnp.float32)[:, None]
        chosen = matches[picked].astype(jnp.float32) * live_float
        route_gate = lax.optimization_barrier(jnp.sum(chosen * gates[picked], axis=1, keepdims=True))
        inputs = jnp.where(is_live[:, None], normalized_tokens[picked], jnp.zeros((), jnp.bfloat16))
        gate_matrix = w_gate[expert_slot]
        up_matrix = w_up[expert_slot]
        down_matrix = w_down[expert_slot]
        gate_pre = jnp.dot(inputs, gate_matrix, preferred_element_type=jnp.float32)
        up_pre = jnp.dot(inputs, up_matrix, preferred_element_type=jnp.float32)
        sigmoid_gate = jax.nn.sigmoid(gate_pre)
        act = (gate_pre * sigmoid_gate * up_pre).astype(jnp.bfloat16)
        expert_out = jnp.dot(act, down_matrix, preferred_element_type=jnp.float32).astype(jnp.bfloat16)
        out_float = expert_out.astype(jnp.float32)
        out_sum = out_sum.at[picked].add(route_gate * out_float)
        picked_grad = cotangent[picked]
        gate_grad = gate_grad.at[picked].add(chosen * lax.optimization_barrier(jnp.sum(picked_grad * out_float, axis=1, keepdims=True)))
        grad_route = (route_gate * picked_grad).astype(jnp.bfloat16)
        grad_act = jnp.dot(grad_route, down_matrix.T, preferred_element_type=jnp.float32)
        grad_gate_pre = (grad_act * up_pre * sigmoid_gate * (1.0 + gate_pre * (1.0 - sigmoid_gate))).astype(jnp.bfloat16)
        grad_up_pre = (grad_act * gate_pre * sigmoid_gate).astype(jnp.bfloat16)
        grad_down = jnp.dot(act.T, grad_route, preferred_element_type=jnp.float32).astype(jnp.bfloat16)
        grad_gate = jnp.dot(inputs.T, grad_gate_pre, preferred_element_type=jnp.float32).astype(jnp.bfloat16)
        grad_up = jnp.dot(inputs.T, grad_up_pre, preferred_element_type=jnp.float32).astype(jnp.bfloat16)
        partial_value = (jnp.dot(grad_gate_pre, gate_matrix.T, preferred_element_type=jnp.float32) + jnp.dot(grad_up_pre, up_matrix.T, preferred_element_type=jnp.float32)).astype(jnp.bfloat16)
        grad_sum = grad_sum.at[picked].add(partial_value.astype(jnp.float32))
        return ((out_sum, grad_sum, gate_grad), (grad_gate, grad_up, grad_down))
    start = (jnp.zeros((TOKENS, D), jnp.float32), jnp.zeros((TOKENS, D), jnp.float32), jnp.zeros((TOKENS, TOP), jnp.float32))
    totals, stacked = lax.scan(per_expert, start, jnp.arange(EXPERTS, dtype=jnp.int32))
    out_sum, normalized_gradient, grad_gates = totals
    grad_w_gate, grad_w_up, grad_w_down = stacked
    gain_gradient = lax.optimization_barrier(jnp.sum(normalized_gradient * unit_scaled_input, axis=0))
    scaled_tokens = normalized_gradient * gain
    token_gradient = (inverse_root_mean * (scaled_tokens - unit_scaled_input * lax.optimization_barrier(jnp.mean(scaled_tokens * unit_scaled_input, axis=1, keepdims=True)))).astype(jnp.bfloat16)
    return (out_sum.astype(jnp.bfloat16), token_gradient, grad_gates, gain_gradient, grad_w_gate, grad_w_up, grad_w_down)
```

```python
import jax
import jax.numpy as jnp
from jax import lax
from jax.sharding import Mesh, PartitionSpec as P


LINE = "line"
PLANE = ("dp", "side")
ALL = ("dp", "line", "side")
F32 = jnp.float32
BF16 = jnp.bfloat16


def dot(left, right, left_dim, right_dim):
    return lax.dot_general(
        left, right, (((left_dim,), (right_dim,)), ((), ())), preferred_element_type=F32
    )


def along_line(value, count, sign):
    return [
        lax.ppermute(value[d] if isinstance(value, list) else value, LINE,
                     [(i, (i + sign * d) % count) for i in range(count)])
        for d in range(1, count)
    ]


def in_plane(rows):
    return lax.all_to_all(rows, PLANE, split_axis=0, concat_axis=0, tiled=True)


def body(tokens, gain, gates, expert_ids, w_gate, w_up, w_down, grad_out):
    rows, top = gates.shape
    width = tokens.shape[1]
    dp_count, line_count, side_count = (lax.axis_size(name) for name in ALL)
    plane_count = dp_count * side_count
    expert_count = plane_count * line_count
    cap = 2 * rows * top // expert_count
    line_rows = line_count * rows
    slots = plane_count * line_count * cap
    place = lax.axis_index(LINE)

    gate_matrix, up_matrix, down_matrix = w_gate[0], w_up[0], w_down[0]

    table = jnp.concatenate([expert_ids.astype(F32).T, gates.T], axis=0)
    tables = jnp.stack([table] + along_line(table, line_count, 1))
    token_blocks = [tokens] + along_line(tokens, line_count, 1)
    grad_blocks = [grad_out] + along_line(grad_out, line_count, 1)

    ids = tables[:, :top]
    block_gates = tables[:, top:]
    plane_index = jnp.arange(plane_count, dtype=jnp.int32)
    plane_expert = (
        (plane_index // side_count) * (line_count * side_count)
        + place * side_count
        + plane_index % side_count
    ).astype(F32)
    named = (ids[:, None] == plane_expert[None, :, None, None]).astype(F32)
    present = jnp.sum(named, axis=2)
    gate_of = jnp.sum(named * block_gates[:, None], axis=2)
    order = jnp.arange(rows, dtype=jnp.int32)
    before = (order[:, None] < order[None, :]).astype(BF16)
    rank = dot(present.astype(BF16).reshape(line_count * plane_count, rows), before, 1, 0)
    code = jnp.where(present > 0.0, rank.reshape(line_count, plane_count, rows), -1.0)
    slot_of = jnp.arange(cap, dtype=jnp.int32).astype(F32)
    hit = code.transpose(1, 0, 2)[:, :, None, :] == slot_of[None, None, :, None]
    same = jnp.eye(line_count, dtype=jnp.bool_)
    picks = (hit[:, :, :, None, :] & same[None, :, None, :, None]).reshape(slots, line_rows)
    pick = picks.astype(BF16)
    gate_rows = gate_of.transpose(1, 0, 2)
    slot_gate = jnp.sum(jnp.where(hit, gate_rows[:, :, None, :], 0.0), axis=3).reshape(slots, 1)
    weights = jnp.where(
        picks.reshape(plane_count, line_count, cap, line_rows),
        gate_rows.reshape(plane_count, 1, 1, line_rows),
        0.0,
    ).reshape(slots, line_rows)

    line_tokens = jnp.concatenate(token_blocks, axis=0)
    line_grads = jnp.concatenate(grad_blocks, axis=0)
    widened = line_tokens.astype(F32)
    inverse_root_mean = lax.rsqrt(jnp.mean(widened * widened, axis=1, keepdims=True) + 1e-06)
    unit_scaled = widened * inverse_root_mean
    normed = (unit_scaled * gain).astype(BF16)

    outgoing = dot(pick, normed, 1, 0).astype(BF16)
    arrived = in_plane(outgoing)
    grad_outgoing = (dot(pick, line_grads, 1, 0) * slot_gate).astype(BF16)
    grad_route = in_plane(grad_outgoing)

    gate_pre = dot(arrived, gate_matrix, 1, 0)
    up_pre = dot(arrived, up_matrix, 1, 0)
    sigmoid_gate = jax.nn.sigmoid(gate_pre)
    act = (gate_pre * sigmoid_gate * up_pre).astype(BF16)
    expert_out = dot(act, down_matrix, 1, 0).astype(BF16)
    returned = in_plane(expert_out)

    grad_act = dot(grad_route, down_matrix, 1, 1)
    grad_gate_pre = (
        grad_act * up_pre * sigmoid_gate * (1.0 + gate_pre * (1.0 - sigmoid_gate))
    ).astype(BF16)
    grad_up_pre = (grad_act * gate_pre * sigmoid_gate).astype(BF16)
    partial_value = (
        dot(grad_gate_pre, gate_matrix, 1, 1) + dot(grad_up_pre, up_matrix, 1, 1)
    ).astype(BF16)
    partial_back = in_plane(partial_value)

    grad_down = dot(act, grad_route, 0, 0).astype(BF16)
    grad_gate = dot(arrived, grad_gate_pre, 0, 0).astype(BF16)
    grad_up = dot(arrived, grad_up_pre, 0, 0).astype(BF16)

    def home(value):
        blocks = value.reshape(line_count, rows, value.shape[1])
        sent = [None] + [blocks[d].astype(BF16) for d in range(1, line_count)]
        total = blocks[0]
        for block in along_line(sent, line_count, -1):
            total = total + block.astype(F32)
        return total

    weights_high = weights.astype(BF16)
    weights_low = (weights - weights_high.astype(F32)).astype(BF16)
    moe_line = dot(weights_high, returned, 0, 0) + dot(weights_low, returned, 0, 0)
    moe_out = home(moe_line).astype(BF16)

    products = dot(line_grads, returned, 1, 1)
    kept = jnp.where(picks, products.T, 0.0).reshape(plane_count, line_count * cap, line_rows)
    per_expert = jnp.sum(kept, axis=1).reshape(plane_count, line_count, rows)
    gate_line = jnp.sum(named * per_expert.transpose(1, 0, 2)[:, :, None, :], axis=1)
    gate_total = gate_line[0]
    for block in along_line([gate_line[d] for d in range(line_count)], line_count, -1):
        gate_total = gate_total + block
    grad_gates = gate_total.T

    normed_line = dot(pick, partial_back, 0, 0)
    normalized_gradient = home(normed_line)
    gain_part = jnp.sum(normed_line * unit_scaled, axis=0)
    gain_parts = lax.all_to_all(
        jnp.broadcast_to(gain_part[None], (expert_count, width)), ALL, 0, 0, tiled=True
    )
    gain_gradient = jnp.sum(gain_parts, axis=0)

    own_unit = unit_scaled[:rows]
    scaled_tokens = normalized_gradient * gain
    token_gradient = (
        inverse_root_mean[:rows]
        * (scaled_tokens - own_unit * jnp.mean(scaled_tokens * own_unit, axis=1, keepdims=True))
    ).astype(BF16)
    return (
        moe_out,
        token_gradient,
        grad_gates,
        gain_gradient,
        grad_gate[None],
        grad_up[None],
        grad_down[None],
    )


def solution(mesh):
    dp_count, expert_count = mesh.devices.shape
    split = Mesh(mesh.devices.reshape(dp_count, expert_count // 2, 2), ALL)
    two, three = P(ALL, None), P(ALL, None, None)
    return jax.shard_map(
        body,
        mesh=split,
        in_specs=(two, P(), two, two, three, three, three, two),
        out_specs=(two, two, two, P(), three, three, three),
        check_vma=False,
    )
```

```python
import jax
import jax.numpy as jnp
from jax import lax
from jax.sharding import Mesh, PartitionSpec as P


LINE = "line"
PLANE = ("dp", "side")
ALL = ("dp", "line", "side")
F32 = jnp.float32
BF16 = jnp.bfloat16


def dot(left, right, left_dim, right_dim):
    return lax.dot_general(
        left, right, (((left_dim,), (right_dim,)), ((), ())), preferred_element_type=F32
    )


def along_line(value, count, sign):
    return [
        lax.ppermute(value[d - 1] if isinstance(value, list) else value, LINE,
                     [(i, (i + sign * d) % count) for i in range(count)])
        for d in range(1, count)
    ]


def in_plane(rows):
    return lax.all_to_all(rows, PLANE, split_axis=0, concat_axis=0, tiled=True)


def normalize(block, gain):
    widened = block.astype(F32)
    inverse = lax.rsqrt(jnp.mean(widened * widened, axis=1, keepdims=True) + 1e-06)
    unit = widened * inverse
    return inverse, unit, (unit * gain).astype(BF16)


def routing(ids, block_gates, plane_expert, cap):
    blocks, _, rows = ids.shape
    planes = plane_expert.shape[0]
    named = (ids[:, None] == plane_expert[None, :, None, None]).astype(F32)
    present = jnp.sum(named, axis=2)
    gate_of = jnp.sum(named * block_gates[:, None], axis=2)
    order = jnp.arange(rows, dtype=jnp.int32)
    before = (order[:, None] < order[None, :]).astype(BF16)
    rank = dot(present.astype(BF16).reshape(blocks * planes, rows), before, 1, 0)
    code = jnp.where(present > 0.0, rank.reshape(blocks, planes, rows), -1.0)
    slot_of = jnp.arange(cap, dtype=jnp.int32).astype(F32)
    hit = code.transpose(1, 0, 2)[:, :, None, :] == slot_of[None, None, :, None]
    same = jnp.eye(blocks, dtype=jnp.bool_)
    shape = (planes * blocks * cap, blocks * rows)
    pick = (hit[:, :, :, None, :] & same[None, :, None, :, None]).reshape(shape)
    gate_rows = gate_of.transpose(1, 0, 2)
    slot_gate = jnp.sum(jnp.where(hit, gate_rows[:, :, None, :], 0.0), axis=3)
    weights = jnp.where(
        pick.reshape(planes, blocks * cap, blocks * rows),
        gate_rows.reshape(planes, 1, blocks * rows),
        0.0,
    ).reshape(shape)
    high = weights.astype(BF16)
    low = (weights - high.astype(F32)).astype(BF16)
    return named, pick, pick.astype(BF16), slot_gate.reshape(-1, 1), high, low


def weigh(route, grads, returned, blocks, cap):
    (named, mask, _, _, high, low), returned = lax.optimization_barrier((route, returned))
    planes = named.shape[1]
    total = dot(high, returned, 0, 0) + dot(low, returned, 0, 0)
    products = dot(returned, grads, 1, 1)
    kept = jnp.where(mask, products, 0.0).reshape(planes, blocks * cap, grads.shape[0])
    per_expert = jnp.sum(kept, axis=1).reshape(planes, blocks, -1).transpose(1, 0, 2)
    return total, jnp.sum(named * per_expert[:, :, None, :], axis=1)


def compute(tokens, gain, gates, expert_ids, w_gate, w_up, w_down, grad_out):
    rows, top = gates.shape
    width = tokens.shape[1]
    dp_count, line_count, side_count = (lax.axis_size(name) for name in ALL)
    plane_count = dp_count * side_count
    expert_count = plane_count * line_count
    cap = 2 * rows * top // expert_count
    far = line_count - 1
    own_slots = plane_count * cap
    place = lax.axis_index(LINE)

    gate_matrix, up_matrix, down_matrix = w_gate[0], w_up[0], w_down[0]

    table = jnp.concatenate([expert_ids.astype(F32).T, gates.T], axis=0)
    far_tables = jnp.stack(along_line(table, line_count, 1))
    token_blocks = along_line(tokens, line_count, 1)
    grad_blocks = along_line(grad_out, line_count, 1)

    plane_index = jnp.arange(plane_count, dtype=jnp.int32)
    plane_expert = (
        (plane_index // side_count) * (line_count * side_count)
        + place * side_count
        + plane_index % side_count
    ).astype(F32)
    own_route = routing(table[None, :top], table[None, top:], plane_expert, cap)
    far_route = routing(far_tables[:, :top], far_tables[:, top:], plane_expert, cap)

    own_inverse, own_unit, own_normed = normalize(tokens, gain)
    own_send = jnp.concatenate(
        [
            dot(own_route[2], own_normed, 1, 0).astype(BF16),
            (dot(own_route[2], grad_out, 1, 0) * own_route[3]).astype(BF16),
        ],
        axis=1,
    )
    own_arrived = in_plane(own_send)

    far_tokens = jnp.concatenate(token_blocks, axis=0)
    far_grads = jnp.concatenate(grad_blocks, axis=0)
    _, far_unit, far_normed = normalize(far_tokens, gain)
    far_arrived = in_plane(dot(far_route[2], far_normed, 1, 0).astype(BF16))
    far_grad_route = in_plane((dot(far_route[2], far_grads, 1, 0) * far_route[3]).astype(BF16))

    arrived = jnp.concatenate([own_arrived[:, :width], far_arrived], axis=0)

    gate_pre = dot(arrived, gate_matrix, 1, 0)
    up_pre = dot(arrived, up_matrix, 1, 0)
    sigmoid_gate = jax.nn.sigmoid(gate_pre)
    act = (gate_pre * sigmoid_gate * up_pre).astype(BF16)
    far_out = dot(act[own_slots:], down_matrix, 1, 0).astype(BF16)
    far_returned = in_plane(far_out)

    gate_pre, up_pre, far_grad_route = lax.optimization_barrier((gate_pre, up_pre, far_grad_route))
    sigmoid_gate = jax.nn.sigmoid(gate_pre)
    grad_route = jnp.concatenate([own_arrived[:, width:], far_grad_route], axis=0)
    grad_act = dot(grad_route, down_matrix, 1, 1)
    grad_gate_pre = (
        grad_act * up_pre * sigmoid_gate * (1.0 + gate_pre * (1.0 - sigmoid_gate))
    ).astype(BF16)
    grad_up_pre = (grad_act * gate_pre * sigmoid_gate).astype(BF16)

    def back(cut):
        return (
            dot(grad_gate_pre[cut], gate_matrix, 1, 1) + dot(grad_up_pre[cut], up_matrix, 1, 1)
        ).astype(BF16)

    far_back = in_plane(back(slice(own_slots, None)))
    own_out = dot(act[:own_slots], down_matrix, 1, 0).astype(BF16)
    own_returned = in_plane(jnp.concatenate([own_out, back(slice(0, own_slots))], axis=1))

    grad_down = dot(act, grad_route, 0, 0).astype(BF16)
    grad_gate = dot(arrived, grad_gate_pre, 0, 0).astype(BF16)
    grad_up = dot(arrived, grad_up_pre, 0, 0).astype(BF16)

    def homeward(value):
        sent = [value[d * rows : (d + 1) * rows].astype(BF16) for d in range(far)]
        return sum(block.astype(F32) for block in along_line(sent, line_count, -1))

    far_moe, far_gate = weigh(far_route, far_grads, far_returned, far, cap)
    moe_home = homeward(far_moe)
    gate_home = sum(along_line([far_gate[d] for d in range(far)], line_count, -1))

    far_normed_sum = dot(far_route[2], far_back, 0, 0)
    back_home = homeward(far_normed_sum)
    far_gain = jnp.sum(far_normed_sum * far_unit, axis=0)

    own_moe, own_gate = weigh(own_route, grad_out, own_returned[:, :width], 1, cap)
    moe_out = (own_moe + moe_home).astype(BF16)
    grad_gates = (own_gate[0] + gate_home).T
    own_normed_sum = dot(own_route[2], own_returned[:, width:], 0, 0)
    gain_part = far_gain + jnp.sum(own_normed_sum * own_unit, axis=0)
    late_gain, gain_part = lax.optimization_barrier((gain, gain_part))
    gain_parts = lax.all_to_all(
        jnp.broadcast_to(gain_part[None], (expert_count, width)), ALL, 0, 0, tiled=True
    )
    gain_gradient = jnp.sum(gain_parts, axis=0)

    normalized_gradient = own_normed_sum + back_home
    scaled_tokens = normalized_gradient * late_gain
    token_gradient = (
        own_inverse
        * (scaled_tokens - own_unit * jnp.mean(scaled_tokens * own_unit, axis=1, keepdims=True))
    ).astype(BF16)
    return (
        moe_out,
        token_gradient,
        grad_gates,
        gain_gradient,
        grad_gate[None],
        grad_up[None],
        grad_down[None],
    )


def solution(mesh):
    dp_count, expert_count = mesh.devices.shape
    split = Mesh(mesh.devices.reshape(dp_count, expert_count // 2, 2), ALL)
    two, three = P(ALL, None), P(ALL, None, None)
    return jax.shard_map(
        compute,
        mesh=split,
        in_specs=(two, P(), two, two, three, three, three, two),
        out_specs=(two, two, two, P(), three, three, three),
        check_vma=False,
    )
```
